256 devices in a mesh: mom: 16 (over z, core), bond: 16 (over y, x).
Axes of the slice: x: 4, y: 4, z: 8, core: 2. Of those that a mesh axis runs over, the one named last changes fastest.
Arguments:
- vertex: bfloat16 [3, 256, 512, 512], P(None, ('mom', 'bond')), may hold values from -6 to 6
- loop_matrix: bfloat16 [3, 256, 512, 512], P(None, ('mom', 'bond')), may hold values from -0.01171875 to 0.01171875
- own_mix: float32 [3, 3], replicated, may hold values from -4 to 4
- cross_mix: float32 [3, 3], replicated, may hold values from -4 to 4
- shells: int32 [512], replicated, may hold values from 0 to 4
- partner: int32 [512], replicated, may hold values from 0 to 511, as said below
- grid_index: int32 [256], replicated, may hold values from 0 to 255, each once
Outputs:
- flowed: bfloat16 [3, 256, 512, 512], P(None, ('mom', 'bond'))
The draws below stay inside these ranges and needn't reach their ends.
Inputs may be any that keep to these rules, and one draw needn't show every extreme that they name: partner[partner[a]] = a and partner[a] != a for every bond a; partner[a] // 32 = (a // 32 + 512 // 64) % 16. `grid_index`: each grid point appears once; point k has coordinates (k // 16, k % 16).
All inputs are finite; a program needn't handle non-finite values.
Results may differ from the reference program's by a relative error of at most 0.007.
Values may be sent and summed in bfloat16 or wider, within the bound.
No kernel may reach another device: no remote copies, remote signals or barrier semaphores. Data moves between devices by JAX's collectives and lax.ppermute only.
A program may use at most 128 MiB of HBM per device.

```python
import math
import jax
import jax.numpy as jnp
from jax import lax

G = 16
NB = 512
NCH = 3
SHELLS = 5
Q = 256
PB = 32


def draw_partner(key, part):
    half_blocks = NB // PB // 2
    scores = jax.random.randint(key, (half_blocks, PB), 0, 1 << 20) * PB + jnp.arange(PB, dtype=jnp.int32)[None, :]
    sigma_order = jnp.argsort(scores, axis=1).astype(jnp.int32)
    inverse = jnp.argsort(sigma_order, axis=1).astype(jnp.int32)
    block_ids = jnp.arange(half_blocks, dtype=jnp.int32)[:, None]
    lower_half = (block_ids + half_blocks) * PB + sigma_order
    upper_half = block_ids * PB + inverse
    return jnp.concatenate([lower_half.reshape(-1), upper_half.reshape(-1)]).astype(jnp.int32)


def place_ends(values, key, smallest, top_value):
    extent = values.shape
    index_at = [jax.random.randint(jax.random.fold_in(key, axis), (), 0, extent[axis]) for axis in range(len(extent))]
    values = values.at[tuple(index_at)].set(smallest)
    longest = extent.index(max(extent))
    index_at[longest] = (index_at[longest] + 1) % extent[longest]
    return values.at[tuple(index_at)].set(top_value)


def block_scale(key, extent, cuts, least, top_value):
    gain, own = 1.0, jax.random.fold_in(key, 6)
    for dim, blocks in cuts:
        draws = jnp.exp(jax.random.uniform(jax.random.fold_in(own, dim), (blocks,), jnp.float32, least / len(cuts), top_value / len(cuts)))
        gain = gain * jnp.repeat(draws, extent[dim] // blocks).reshape([-1 if axis == dim else 1 for axis in range(len(extent))])
    return gain


def noise(stream_key, dims, width, limit, cuts=(), held_as=jnp.bfloat16):
    loudness = block_scale(stream_key, dims, cuts, -0.22, 0.18) if cuts else 1.0
    result = jax.random.normal(stream_key, dims, jnp.float32) * width * loudness
    return jnp.minimum(jnp.maximum(result, -limit), limit).astype(held_as)


def setup_inputs(seed: int = 0) -> dict:
    key_list = jax.random.split(jax.random.key(seed), 8)
    vertex = noise(key_list[0], (NCH, Q, NB, NB), 1.0, 6.0, ((1, 256),))
    loop_matrix = noise(key_list[1], (NCH, Q, NB, NB), (NB * NB) ** -0.5, 0.01171875, ((1, 256),))
    own_mix = noise(key_list[2], (NCH, NCH), 1.0, 4.0, (), jnp.float32)
    cross_mix = noise(key_list[3], (NCH, NCH), 1.0, 4.0, (), jnp.float32)
    shells = place_ends(jax.random.randint(key_list[4], (NB,), 0, SHELLS), jax.random.fold_in(key_list[4], 1), 0, SHELLS - 1).astype(jnp.int32)
    partner = draw_partner(jax.random.fold_in(key_list[7], 71), 0)
    grid_index = jax.random.permutation(key_list[6], Q).astype(jnp.int32)
    return {"vertex": vertex, "loop_matrix": loop_matrix, "own_mix": own_mix, "cross_mix": cross_mix, "shells": shells, "partner": partner, "grid_index": grid_index}


def cas_table(grid_index, negate):
    points = jnp.arange(Q, dtype=jnp.int32)
    disp_x = points // G
    disp_y = points % G
    wave_x = grid_index // G
    wave_y = grid_index % G
    phases = (disp_x[:, None] * wave_x[None, :] + disp_y[:, None] * wave_y[None, :]) % G
    if negate:
        phases = (G - phases) % G
    angles = phases.astype(jnp.float32) * (2.0 * math.pi / G)
    return (jnp.cos(angles) + jnp.sin(angles)).astype(jnp.bfloat16)


def cycle_index():
    points = jnp.arange(Q, dtype=jnp.int32)
    centre_x = (points // G + G // 2) % G - G // 2
    centre_y = (points % G + G // 2) % G - G // 2
    return jnp.maximum(jnp.abs(centre_x), jnp.abs(centre_y))


def reference(vertex, loop_matrix, own_mix, cross_mix, shells, partner, grid_index):
    def flow_step(operands):
        vertex_one, loop_one = operands
        vertex_wide = vertex_one.astype(jnp.float32)
        half_product = jnp.einsum("qab,qbd->qad", vertex_wide, loop_one.astype(jnp.float32)).astype(jnp.bfloat16)
        return jnp.einsum("qab,qbd->qad", half_product.astype(jnp.float32), vertex_wide)

    product = lax.map(flow_step, (vertex, loop_matrix))
    rounded = product.astype(jnp.bfloat16)
    crossed = jnp.take(jnp.take(rounded, partner, axis=2), partner, axis=3)
    plus_table = cas_table(grid_index, False).astype(jnp.float32)
    minus_table = cas_table(grid_index, True).astype(jnp.float32)
    cycle_values = cycle_index()
    height = math.gcd(NB, 64)
    block_count = NB // height
    row_width = height * NB

    def by_rows(field_data):
        return jnp.moveaxis(field_data.reshape(NCH, Q, block_count, height, NB), 2, 0)

    def lattice_step(operands):
        own_rows, cross_rows, shell_rows = operands
        own_lattice = jnp.einsum("rq,cqe->cre", plus_table, own_rows.reshape(NCH, Q, row_width).astype(jnp.float32), precision=lax.Precision.HIGHEST)
        cross_lattice = jnp.einsum("rq,cqe->cre", minus_table, cross_rows.reshape(NCH, Q, row_width).astype(jnp.float32), precision=lax.Precision.HIGHEST)
        mixed_terms = jnp.einsum("dc,cre->dre", own_mix, own_lattice, precision=lax.Precision.HIGHEST) + jnp.einsum("dc,cre->dre", cross_mix, cross_lattice, precision=lax.Precision.HIGHEST)
        reach_sum = (shell_rows[:, None] + shells[None, :]).reshape(row_width)
        kept_mask = cycle_values[:, None] <= reach_sum[None, :]
        projected = jnp.where(kept_mask[None], mixed_terms * (1.0 / Q), 0.0).astype(jnp.bfloat16)
        returned = jnp.einsum("rq,dre->dqe", plus_table, projected.astype(jnp.float32), precision=lax.Precision.HIGHEST)
        return returned.astype(jnp.bfloat16)

    pieces = lax.map(lattice_step, (by_rows(rounded), by_rows(crossed), shells.reshape(block_count, height)))
    returned = jnp.moveaxis(pieces.reshape(block_count, NCH, Q, height, NB), 0, 2).reshape(NCH, Q, NB, NB)
    flowed = vertex.astype(jnp.float32) + product + returned.astype(jnp.float32)
    return flowed.astype(jnp.bfloat16)
```

```python
import math

import jax
import jax.numpy as jnp
from jax import lax
from jax.experimental import pallas as pl
from jax.experimental.pallas import tpu as pltpu
from jax.sharding import PartitionSpec as P

G = 16
NB = 512
Q = 256
NCH = 3
HALF = NB // 2
SUB = 8
LANES = 128
TILE_COLS = NB // LANES
PAIR = SUB // 2
AXES = ("mom", "bond")

CAS = [math.cos(2 * math.pi * n / G) + math.sin(2 * math.pi * n / G) for n in range(8)]
CAS[6] = 0.0


def iota(shape, dim):
    return lax.broadcasted_iota(jnp.int32, shape, dim)


def orbit_select(partner_row):
    row = iota((NB, NB), 0)
    bond = (row // SUB) * PAIR + row % PAIR
    source = jnp.where(row % SUB < PAIR, iota((NB, NB), 1), partner_row)
    return (source == bond).astype(jnp.float32)


def partner_matrix(partner_row):
    return (partner_row == iota((NB, NB), 0)).astype(jnp.float32)


def dot(a, b):
    return jnp.dot(a, b, preferred_element_type=jnp.float32)


def product_kernel(vertex_ref, loop_ref, partner_ref, sent_ref, sum_ref, swap_ref, select_ref):
    @pl.when(pl.program_id(0) == 0)
    def _():
        partner_row = partner_ref[...]
        swap_ref[...] = partner_matrix(partner_row).astype(jnp.bfloat16)
        select_ref[...] = orbit_select(partner_row).astype(jnp.bfloat16)

    vertex = vertex_ref[0, 0]
    half_product = dot(vertex, loop_ref[0, 0]).astype(jnp.bfloat16)
    product = dot(half_product, vertex)
    sum_ref[0] = vertex.astype(jnp.float32) + product
    rounded = product.astype(jnp.bfloat16)
    lower = dot(rounded[HALF:], swap_ref[...]).astype(jnp.bfloat16)
    ordered = dot(select_ref[...], jnp.concatenate([rounded[:HALF], lower], axis=0))
    for j in range(TILE_COLS):
        piece = ordered[:, j * LANES : (j + 1) * LANES].reshape(NB // SUB, SUB, LANES)
        sent_ref[:, j, 0] = piece.astype(jnp.bfloat16)


def cas_values(phase):
    low = phase & 7
    value = jnp.full(phase.shape, CAS[0], jnp.float32)
    for n in range(1, 8):
        value = jnp.where(low == n, CAS[n], value)
    return jnp.where(phase & 8 != 0, -value, value)


def lattice_kernel(
    place_ref, own_mix_ref, cross_mix_ref, shells_s, partner_s, arrived_ref, grid_ref, shells_ref, partner_ref,
    back_ref, in_ref, out_ref,
):
    place = place_ref[0]
    tile_row = place // TILE_COLS
    tile_col = place % TILE_COLS
    shape = (Q, Q)
    point = grid_ref[...]
    disp = iota(shape, 0)
    phase = (disp // G) * (point // G) + (disp % G) * (point % G)
    plus = cas_values(phase & 15)
    minus = cas_values((-phase) & 15)
    plus_back = plus.T.astype(jnp.bfloat16)
    tables = jnp.concatenate([plus, minus], axis=0).astype(jnp.bfloat16)

    shell_row = shells_ref[pl.ds(tile_col, 1), :]
    pick = (iota((NB, LANES), 0) == partner_ref[pl.ds(tile_col, 1), :]).astype(jnp.float32).astype(jnp.bfloat16)
    crossed_row = jnp.zeros((SUB, LANES), jnp.float32)
    for j in range(TILE_COLS):
        part = jnp.broadcast_to(shells_ref[pl.ds(j, 1), :], (SUB, LANES)).astype(jnp.float32).astype(jnp.bfloat16)
        crossed_row += dot(part, pick[j * LANES : (j + 1) * LANES])
    crossed_shell_row = crossed_row[:1].astype(jnp.int32)
    lattice_point = iota((Q, LANES), 0)
    centre_x = (lattice_point // G + G // 2) % G - G // 2
    centre_y = (lattice_point % G + G // 2) % G - G // 2
    cycle = jnp.maximum(jnp.abs(centre_x), jnp.abs(centre_y))

    for c in range(NCH):
        in_ref[c] = arrived_ref[:, c].astype(jnp.float32).reshape(Q * SUB, LANES)
    for s in range(PAIR):
        bond = tile_row * PAIR + s
        own_keep = cycle <= shell_row + shells_s[bond]
        cross_keep = cycle <= crossed_shell_row + shells_s[partner_s[bond]]
        lattice = []
        for c in range(NCH):
            own = in_ref[c, pl.ds(s, Q, stride=SUB), :].astype(jnp.bfloat16)
            crossed = in_ref[c, pl.ds(s + PAIR, Q, stride=SUB), :].astype(jnp.bfloat16)
            lattice.append(dot(tables, jnp.concatenate([own, crossed], axis=1)))
        for d in range(NCH):
            own_sum = jnp.zeros((Q, LANES), jnp.float32)
            cross_sum = jnp.zeros((Q, LANES), jnp.float32)
            for c in range(NCH):
                own_gain = own_mix_ref[d, c] * (1.0 / Q)
                cross_gain = cross_mix_ref[d, c] * (1.0 / Q)
                own_sum += own_gain * lattice[c][:Q, :LANES] + cross_gain * lattice[c][Q:, LANES:]
                cross_sum += own_gain * lattice[c][:Q, LANES:] + cross_gain * lattice[c][Q:, :LANES]
            projected = jnp.concatenate(
                [jnp.where(own_keep, own_sum, 0.0), jnp.where(cross_keep, cross_sum, 0.0)], axis=1
            ).astype(jnp.bfloat16)
            returned = dot(plus_back, projected)
            out_ref[d, pl.ds(s, Q, stride=SUB), :] = returned[:, :LANES]
            out_ref[d, pl.ds(s + PAIR, Q, stride=SUB), :] = returned[:, LANES:]
    for d in range(NCH):
        back_ref[:, d] = out_ref[d].reshape(Q, SUB, LANES).astype(jnp.bfloat16)


def flow_kernel(back_ref, sum_ref, partner_ref, flowed_ref, swap_ref, select_ref):
    @pl.when(pl.program_id(0) == 0)
    def _():
        partner_row = partner_ref[...]
        swap_ref[...] = partner_matrix(partner_row).astype(jnp.bfloat16)
        select_ref[...] = orbit_select(partner_row).T.astype(jnp.bfloat16)

    columns = [
        back_ref[:, j, 0].astype(jnp.float32).reshape(NB, LANES).astype(jnp.bfloat16) for j in range(TILE_COLS)
    ]
    returned = dot(select_ref[...], jnp.concatenate(columns, axis=1))
    lower = dot(returned[HALF:].astype(jnp.bfloat16), swap_ref[...])
    flowed_ref[0, 0, :HALF] = (sum_ref[0, :HALF] + returned[:HALF]).astype(jnp.bfloat16)
    flowed_ref[0, 0, HALF:] = (sum_ref[0, HALF:] + lower).astype(jnp.bfloat16)


def per_device(vertex, loop_matrix, own_mix, cross_mix, shells, partner, grid_index):
    f32, bf16 = jnp.float32, jnp.bfloat16
    tiles = (NB // SUB, TILE_COLS, NCH, SUB, LANES)
    matrix_spec = pl.BlockSpec((1, 1, NB, NB), lambda c: (c, 0, 0, 0))
    tiles_spec = pl.BlockSpec((NB // SUB, TILE_COLS, 1, SUB, LANES), lambda c: (0, 0, c, 0, 0))
    sum_spec = pl.BlockSpec((1, NB, NB), lambda c: (c, 0, 0))
    partner_spec = pl.BlockSpec((1, NB), lambda c: (0, 0))
    selectors = [pltpu.VMEM((NB, NB), bf16), pltpu.VMEM((NB, NB), bf16)]
    params = pltpu.CompilerParams(vmem_limit_bytes=40 << 20)
    partner_row = partner.reshape(1, NB)
    sent, vertex_sum = pl.pallas_call(
        product_kernel,
        grid=(NCH,),
        in_specs=[matrix_spec, matrix_spec, partner_spec],
        out_specs=[tiles_spec, sum_spec],
        out_shape=[jax.ShapeDtypeStruct(tiles, bf16), jax.ShapeDtypeStruct((NCH, NB, NB), f32)],
        scratch_shapes=selectors,
        compiler_params=params,
        name="product",
    )(vertex, loop_matrix, partner_row)
    arrived = lax.all_to_all(sent.reshape(Q, NCH, SUB, LANES), AXES, 0, 0, tiled=True)
    place = lax.axis_index(AXES).astype(jnp.int32).reshape(1)
    smem = pl.BlockSpec(memory_space=pltpu.SMEM)
    vmem = pl.BlockSpec(memory_space=pltpu.VMEM)
    back = pl.pallas_call(
        lattice_kernel,
        in_specs=[smem] * 5 + [vmem] * 4,
        out_specs=vmem,
        out_shape=jax.ShapeDtypeStruct((Q, NCH, SUB, LANES), bf16),
        scratch_shapes=[pltpu.VMEM((NCH, Q * SUB, LANES), f32), pltpu.VMEM((NCH, Q * SUB, LANES), f32)],
        compiler_params=params,
        name="lattice",
    )(
        place, own_mix, cross_mix, shells, partner, arrived,
        grid_index.reshape(1, Q), shells.reshape(TILE_COLS, LANES), partner.reshape(TILE_COLS, LANES),
    )
    received = lax.all_to_all(back, AXES, 0, 0, tiled=True).reshape(tiles)
    return pl.pallas_call(
        flow_kernel,
        grid=(NCH,),
        in_specs=[tiles_spec, sum_spec, partner_spec],
        out_specs=matrix_spec,
        out_shape=jax.ShapeDtypeStruct((NCH, 1, NB, NB), bf16),
        scratch_shapes=selectors,
        compiler_params=params,
        name="flow",
    )(received, vertex_sum, partner_row)


def solution(mesh):
    split = P(None, ("mom", "bond"), None, None)
    return jax.shard_map(
        per_device, mesh=mesh, in_specs=(split, split, P(), P(), P(), P(), P()), out_specs=split, check_vma=False
    )
```

```python
import math

import jax
import jax.numpy as jnp
from jax import lax
from jax.experimental import pallas as pl
from jax.experimental.pallas import tpu as pltpu
from jax.sharding import PartitionSpec as P

G = 16
NB = 512
Q = 256
NCH = 3
HALF = NB // 2
SUB = 8
LANES = 128
TILE_COLS = NB // LANES
PAIR = SUB // 2
TILES = (HALF // SUB, 2, TILE_COLS, NCH, SUB, LANES)
AXES = ("mom", "bond")

CAS = [math.cos(2 * math.pi * n / G) + math.sin(2 * math.pi * n / G) for n in range(8)]
CAS[6] = 0.0

SMEM = pl.BlockSpec(memory_space=pltpu.SMEM)
VMEM = pl.BlockSpec(memory_space=pltpu.VMEM)
HBM = pl.BlockSpec(memory_space=pltpu.HBM)
FULL = pltpu.CompilerParams(vmem_limit_bytes=63 << 20)
PARAMS = pltpu.CompilerParams(vmem_limit_bytes=40 << 20)


def iota(shape, dim):
    return lax.broadcasted_iota(jnp.int32, shape, dim)


def to_bf16(flags):
    return flags.astype(jnp.float32).astype(jnp.bfloat16)


def dot(a, b):
    return jnp.dot(a, b, preferred_element_type=jnp.float32)


def partner_blocks(partner_ref):
    rows = iota((HALF, HALF), 0)
    upper_of = to_bf16(partner_ref[:, HALF:] == rows)
    lower_of = to_bf16(partner_ref[:, :HALF] == rows + HALF)
    return upper_of, lower_of


def swap_columns(x, upper_of, lower_of):
    x = x.astype(jnp.bfloat16)
    return jnp.concatenate([dot(x[:, HALF:], lower_of), dot(x[:, :HALF], upper_of)], axis=1)


def interleave(first, second):
    low = iota(first.shape, 1) < PAIR
    even = jnp.where(low, first, pltpu.roll(second, PAIR, 1))
    odd = jnp.where(low, pltpu.roll(first, PAIR, 1), second)
    return even, odd


def by_groups(x):
    return x.reshape(HALF // SUB, SUB, NB)


def product_of(vertex, loop):
    return dot(dot(vertex, loop).astype(jnp.bfloat16), vertex)


def fetch(pairs, sems):
    copies = [
        [pltpu.make_async_copy(source.at[c, 0], target.at[c], sems.at[i, c]) for i, (source, target) in enumerate(pairs)]
        for c in range(NCH)
    ]
    for group in copies:
        for copy in group:
            copy.start()
    return copies


def product_kernel(vertex_hbm, loop_hbm, partner_ref, sent_hbm, vertex_buf, loop_buf, sems, sent_ref, sent_sems):
    copies = fetch([(vertex_hbm, vertex_buf), (loop_hbm, loop_buf)], sems)
    upper_of, lower_of = partner_blocks(partner_ref)
    sends = []
    for c in range(NCH):
        for copy in copies[c]:
            copy.wait()
        product = product_of(vertex_buf[c], loop_buf[c])
        swapped = swap_columns(product[HALF:], upper_of, lower_of).astype(jnp.bfloat16)
        crossed = dot(upper_of, swapped)
        for half, rows in enumerate(interleave(by_groups(product[:HALF]), by_groups(crossed))):
            for j in range(TILE_COLS):
                sent_ref[:, half, j, c] = rows[:, :, j * LANES : (j + 1) * LANES].astype(jnp.bfloat16)
        sends.append(pltpu.make_async_copy(sent_ref.at[:, :, :, c], sent_hbm.at[:, :, :, c], sent_sems.at[c]))
        sends[c].start()
    for copy in sends:
        copy.wait()


def cas_values(phase):
    low = phase & 7
    value = jnp.full(phase.shape, CAS[0], jnp.float32)
    for n in range(1, 8):
        value = jnp.where(low == n, CAS[n], value)
    return jnp.where(phase & 8 != 0, -value, value)


def side_kernel(
    tile_col_ref, vertex_hbm, loop_hbm, grid_ref, shells_ref, partner_ref, sum_ref, tables_ref, back_ref, shell_rows_ref,
    vertex_buf, loop_buf, sems,
):
    copies = fetch([(vertex_hbm, vertex_buf), (loop_hbm, loop_buf)], sems)
    point = grid_ref[...]
    disp = iota((Q, Q), 0)
    phase = (disp // G) * (point // G) + (disp % G) * (point % G)
    plus = cas_values(phase & 15)
    tables_ref[:Q] = plus.astype(jnp.bfloat16)
    tables_ref[Q:] = cas_values((-phase) & 15).astype(jnp.bfloat16)
    back_ref[...] = plus.T.astype(jnp.bfloat16)
    tile_col = tile_col_ref[0]
    pick = to_bf16(iota((NB, LANES), 0) == partner_ref[pl.ds(tile_col, 1), :])
    crossed_row = jnp.zeros((SUB, LANES), jnp.float32)
    for j in range(TILE_COLS):
        part = to_bf16(jnp.broadcast_to(shells_ref[pl.ds(j, 1), :], (SUB, LANES)))
        crossed_row += dot(part, pick[j * LANES : (j + 1) * LANES])
    own_row = jnp.broadcast_to(shells_ref[pl.ds(tile_col, 1), :], (SUB, LANES))
    shell_rows_ref[...] = jnp.where(iota((SUB, LANES), 0) < PAIR, own_row, crossed_row.astype(jnp.int32))
    for c in range(NCH):
        for copy in copies[c]:
            copy.wait()
        vertex = vertex_buf[c]
        sum_ref[c] = vertex.astype(jnp.float32) + product_of(vertex, loop_buf[c])


def lattice_kernel(
    tile_row_ref, own_mix_ref, cross_mix_ref, shells_s, partner_s, arrived_ref, tables_ref, plus_back_ref,
    shell_rows_ref, back_ref, in_ref, out_ref,
):
    tile_row = tile_row_ref[0]
    lattice_point = iota((Q, LANES), 0)
    centre_x = (lattice_point // G + G // 2) % G - G // 2
    centre_y = (lattice_point % G + G // 2) % G - G // 2
    cycle = jnp.maximum(jnp.abs(centre_x), jnp.abs(centre_y))
    for c in range(NCH):
        in_ref[c] = arrived_ref[:, c].astype(jnp.float32).reshape(Q * SUB, LANES)
    for s in range(PAIR):
        bond = tile_row * PAIR + s
        own_keep = cycle <= shell_rows_ref[0:1, :] + shells_s[bond]
        cross_keep = cycle <= shell_rows_ref[PAIR : PAIR + 1, :] + shells_s[partner_s[bond]]
        lattice = []
        for c in range(NCH):
            own = in_ref[c, pl.ds(s, Q, stride=SUB), :].astype(jnp.bfloat16)
            crossed = in_ref[c, pl.ds(s + PAIR, Q, stride=SUB), :].astype(jnp.bfloat16)
            lattice.append(dot(tables_ref[...], jnp.concatenate([own, crossed], axis=1)))
        for d in range(NCH):
            own_sum = jnp.zeros((Q, LANES), jnp.float32)
            cross_sum = jnp.zeros((Q, LANES), jnp.float32)
            for c in range(NCH):
                own_gain = own_mix_ref[d, c] * (1.0 / Q)
                cross_gain = cross_mix_ref[d, c] * (1.0 / Q)
                own_sum += own_gain * lattice[c][:Q, :LANES] + cross_gain * lattice[c][Q:, LANES:]
                cross_sum += own_gain * lattice[c][:Q, LANES:] + cross_gain * lattice[c][Q:, :LANES]
            projected = jnp.concatenate(
                [jnp.where(own_keep, own_sum, 0.0), jnp.where(cross_keep, cross_sum, 0.0)], axis=1
            ).astype(jnp.bfloat16)
            returned = dot(plus_back_ref[...], projected)
            out_ref[d, pl.ds(s, Q, stride=SUB), :] = returned[:, :LANES]
            out_ref[d, pl.ds(s + PAIR, Q, stride=SUB), :] = returned[:, LANES:]
    for d in range(NCH):
        back_ref[:, d] = out_ref[d].reshape(Q, SUB, LANES).astype(jnp.bfloat16)


def flow_kernel(received_ref, sum_ref, partner_ref, flowed_hbm, flowed_buf, sems):
    upper_of, lower_of = partner_blocks(partner_ref)
    copies = []
    for c in range(NCH):
        halves = [
            jnp.concatenate([received_ref[:, half, j, c].astype(jnp.float32) for j in range(TILE_COLS)], axis=2)
            for half in range(2)
        ]
        own, crossed = interleave(*halves)
        rows = dot(lower_of, crossed.reshape(HALF, NB).astype(jnp.bfloat16))
        lower = swap_columns(rows, upper_of, lower_of)
        flowed_buf[c, :HALF] = (sum_ref[c, :HALF] + own.reshape(HALF, NB)).astype(jnp.bfloat16)
        flowed_buf[c, HALF:] = (sum_ref[c, HALF:] + lower).astype(jnp.bfloat16)
        copies.append(pltpu.make_async_copy(flowed_buf.at[c], flowed_hbm.at[c, 0], sems.at[c]))
        copies[c].start()
    for copy in copies:
        copy.wait()


def per_device(vertex, loop_matrix, own_mix, cross_mix, shells, partner, grid_index):
    f32, bf16, i32 = jnp.float32, jnp.bfloat16, jnp.int32
    shape = jax.ShapeDtypeStruct
    fetched = [
        pltpu.VMEM((NCH, NB, NB), bf16),
        pltpu.VMEM((NCH, NB, NB), bf16),
        pltpu.SemaphoreType.DMA((2, NCH)),
    ]
    partner_row = partner.reshape(1, NB)
    place = lax.axis_index(AXES).astype(i32)
    sent = pl.pallas_call(
        product_kernel,
        in_specs=[HBM, HBM, VMEM],
        out_specs=HBM,
        out_shape=shape(TILES, bf16),
        scratch_shapes=[*fetched, pltpu.VMEM(TILES, bf16), pltpu.SemaphoreType.DMA((NCH,))],
        compiler_params=FULL,
        name="product",
    )(vertex, loop_matrix, partner_row)
    arrived = lax.all_to_all(sent.reshape(Q, NCH, SUB, LANES), AXES, 0, 0, tiled=True)
    vertex_sum, tables, plus_back, shell_rows = pl.pallas_call(
        side_kernel,
        in_specs=[SMEM, HBM, HBM, VMEM, VMEM, VMEM],
        out_specs=[VMEM] * 4,
        out_shape=[shape((NCH, NB, NB), f32), shape((2 * Q, Q), bf16), shape((Q, Q), bf16), shape((SUB, LANES), i32)],
        scratch_shapes=fetched,
        compiler_params=PARAMS,
        name="side",
    )(
        (place % TILE_COLS).reshape(1), vertex, loop_matrix, grid_index.reshape(1, Q),
        shells.reshape(TILE_COLS, LANES), partner.reshape(TILE_COLS, LANES),
    )
    back = pl.pallas_call(
        lattice_kernel,
        in_specs=[SMEM] * 5 + [VMEM] * 4,
        out_specs=VMEM,
        out_shape=shape((Q, NCH, SUB, LANES), bf16),
        scratch_shapes=[pltpu.VMEM((NCH, Q * SUB, LANES), f32), pltpu.VMEM((NCH, Q * SUB, LANES), f32)],
        compiler_params=PARAMS,
        name="lattice",
    )((place // TILE_COLS).reshape(1), own_mix, cross_mix, shells, partner, arrived, tables, plus_back, shell_rows)
    received = lax.all_to_all(back, AXES, 0, 0, tiled=True).reshape(TILES)
    return pl.pallas_call(
        flow_kernel,
        in_specs=[VMEM, VMEM, VMEM],
        out_specs=HBM,
        out_shape=shape((NCH, 1, NB, NB), bf16),
        scratch_shapes=[pltpu.VMEM((NCH, NB, NB), bf16), pltpu.SemaphoreType.DMA((NCH,))],
        compiler_params=PARAMS,
        name="flow",
    )(received, vertex_sum, partner_row)


def solution(mesh):
    split = P(None, ("mom", "bond"), None, None)
    return jax.shard_map(
        per_device, mesh=mesh, in_specs=(split, split, P(), P(), P(), P(), P()), out_specs=split, check_vma=False
    )
```

```python
import math

import jax
import jax.numpy as jnp
from jax import lax
from jax.experimental import pallas as pl
from jax.experimental.pallas import tpu as pltpu
from jax.sharding import PartitionSpec as P

G = 16
NB = 512
Q = 256
NCH = 3
HALF = NB // 2
SUB = 8
LANES = 128
TILE_COLS = NB // LANES
PAIR = SUB // 2
TILES = (HALF // SUB, 2, TILE_COLS, NCH, SUB, LANES)
AXES = ("mom", "bond")
LIMITS = 0
GAINS = LIMITS + SUB
ROWS = GAINS + SUB

CAS = [math.cos(2 * math.pi * n / G) + math.sin(2 * math.pi * n / G) for n in range(8)]
CAS[6] = 0.0

SMEM = pl.BlockSpec(memory_space=pltpu.SMEM)
VMEM = pl.BlockSpec(memory_space=pltpu.VMEM)
HBM = pl.BlockSpec(memory_space=pltpu.HBM)
FULL = pltpu.CompilerParams(vmem_limit_bytes=63 << 20)
PARAMS = pltpu.CompilerParams(vmem_limit_bytes=40 << 20)


def iota(shape, dim):
    return lax.broadcasted_iota(jnp.int32, shape, dim)


def to_bf16(flags):
    return flags.astype(jnp.float32).astype(jnp.bfloat16)


def dot(a, b):
    return jnp.dot(a, b, preferred_element_type=jnp.float32)


def partner_blocks(partner_ref):
    rows = iota((HALF, HALF), 0)
    upper_of = to_bf16(partner_ref[:, HALF:] == rows)
    lower_of = to_bf16(partner_ref[:, :HALF] == rows + HALF)
    return upper_of, lower_of


def swap_columns(x, upper_of, lower_of):
    x = x.astype(jnp.bfloat16)
    return jnp.concatenate([dot(x[:, HALF:], lower_of), dot(x[:, :HALF], upper_of)], axis=1)


def interleave(first, second):
    low = iota(first.shape, 1) < PAIR
    even = jnp.where(low, first, pltpu.roll(second, PAIR, 1))
    odd = jnp.where(low, pltpu.roll(first, PAIR, 1), second)
    return even, odd


def by_groups(x):
    return x.reshape(HALF // SUB, SUB, NB)


def product_of(vertex, loop):
    return dot(dot(vertex, loop).astype(jnp.bfloat16), vertex)


def fetch(pairs, sems):
    copies = [
        [pltpu.make_async_copy(source.at[c, 0], target.at[c], sems.at[i, c]) for i, (source, target) in enumerate(pairs)]
        for c in range(NCH)
    ]
    for group in copies:
        for copy in group:
            copy.start()
    return copies


def product_kernel(vertex_hbm, loop_hbm, partner_ref, sent_hbm, vertex_buf, loop_buf, sems, sent_ref, sent_sems):
    copies = fetch([(vertex_hbm, vertex_buf), (loop_hbm, loop_buf)], sems)
    upper_of, lower_of = partner_blocks(partner_ref)
    sends = []
    for c in range(NCH):
        for copy in copies[c]:
            copy.wait()
        product = product_of(vertex_buf[c], loop_buf[c])
        swapped = swap_columns(product[HALF:], upper_of, lower_of).astype(jnp.bfloat16)
        crossed = dot(upper_of, swapped)
        for half, rows in enumerate(interleave(by_groups(product[:HALF]), by_groups(crossed))):
            for j in range(TILE_COLS):
                sent_ref[:, half, j, c] = rows[:, :, j * LANES : (j + 1) * LANES].astype(jnp.bfloat16)
        sends.append(pltpu.make_async_copy(sent_ref.at[:, :, :, c], sent_hbm.at[:, :, :, c], sent_sems.at[c]))
        sends[c].start()
    for copy in sends:
        copy.wait()


def cas_values(phase):
    low = phase & 7
    value = jnp.full(phase.shape, CAS[0], jnp.float32)
    for n in range(1, 8):
        value = jnp.where(low == n, CAS[n], value)
    return jnp.where(phase & 8 != 0, -value, value)


def gain_lane(crossed, to, source):
    return (crossed * NCH + to) * NCH + source


def side_kernel(
    place_ref, own_mix_ref, cross_mix_ref, shells_s, partner_s, vertex_hbm, loop_hbm, grid_ref, shells_ref, partner_ref,
    sum_ref, squares_ref, rows_ref, vertex_buf, loop_buf, sems,
):
    copies = fetch([(vertex_hbm, vertex_buf), (loop_hbm, loop_buf)], sems)
    tile_row = place_ref[0] // TILE_COLS
    tile_col = place_ref[0] % TILE_COLS
    point = grid_ref[...]
    disp = iota((Q, Q), 0)
    phase = (disp // G) * (point // G) + (disp % G) * (point % G)
    plus = cas_values(phase & 15)
    squares_ref[0] = plus.astype(jnp.bfloat16)
    squares_ref[1] = cas_values((-phase) & 15).astype(jnp.bfloat16)
    squares_ref[2] = plus.T.astype(jnp.bfloat16)
    pick = to_bf16(iota((NB, LANES), 0) == partner_ref[pl.ds(tile_col, 1), :])
    crossed_row = jnp.zeros((SUB, LANES), jnp.float32)
    for j in range(TILE_COLS):
        part = to_bf16(jnp.broadcast_to(shells_ref[pl.ds(j, 1), :], (SUB, LANES)))
        crossed_row += dot(part, pick[j * LANES : (j + 1) * LANES])
    crossed_row = crossed_row[:1]
    own_row = shells_ref[pl.ds(tile_col, 1), :].astype(jnp.float32)
    for s in range(PAIR):
        bond = tile_row * PAIR + s
        rows_ref[LIMITS + s : LIMITS + s + 1, :] = own_row + shells_s[bond].astype(jnp.float32)
        rows_ref[LIMITS + PAIR + s : LIMITS + PAIR + s + 1, :] = (
            crossed_row + shells_s[partner_s[bond]].astype(jnp.float32)
        )
    lane = iota((SUB, LANES), 1)
    gains = jnp.zeros((SUB, LANES), jnp.float32)
    for d in range(NCH):
        for c in range(NCH):
            gains = jnp.where(lane == gain_lane(0, d, c), own_mix_ref[d, c] * (1.0 / Q), gains)
            gains = jnp.where(lane == gain_lane(1, d, c), cross_mix_ref[d, c] * (1.0 / Q), gains)
    rows_ref[GAINS:] = gains
    for c in range(NCH):
        for copy in copies[c]:
            copy.wait()
        vertex = vertex_buf[c]
        sum_ref[c] = vertex.astype(jnp.float32) + product_of(vertex, loop_buf[c])


def lattice_kernel(arrived_ref, squares_ref, rows_ref, back_ref, in_ref, out_ref):
    lattice_point = iota((Q, LANES), 0)
    centre_x = (lattice_point // G + G // 2) % G - G // 2
    centre_y = (lattice_point % G + G // 2) % G - G // 2
    cycle = jnp.maximum(jnp.abs(centre_x), jnp.abs(centre_y)).astype(jnp.float32)
    tables = squares_ref[:2].reshape(2 * Q, Q)
    gains = rows_ref[GAINS : GAINS + 1, :]
    for c in range(NCH):
        in_ref[c] = arrived_ref[:, c].astype(jnp.float32).reshape(Q * SUB, LANES)
    for s in range(PAIR):
        own_keep = cycle <= rows_ref[LIMITS + s : LIMITS + s + 1, :]
        cross_keep = cycle <= rows_ref[LIMITS + PAIR + s : LIMITS + PAIR + s + 1, :]
        lattice = []
        for c in range(NCH):
            own = in_ref[c, pl.ds(s, Q, stride=SUB), :].astype(jnp.bfloat16)
            crossed = in_ref[c, pl.ds(s + PAIR, Q, stride=SUB), :].astype(jnp.bfloat16)
            lattice.append(dot(tables, jnp.concatenate([own, crossed], axis=1)))
        for d in range(NCH):
            own_sum = jnp.zeros((Q, LANES), jnp.float32)
            cross_sum = jnp.zeros((Q, LANES), jnp.float32)
            for c in range(NCH):
                at = gain_lane(0, d, c)
                own_gain = gains[:, at : at + 1]
                at = gain_lane(1, d, c)
                cross_gain = gains[:, at : at + 1]
                own_sum += own_gain * lattice[c][:Q, :LANES] + cross_gain * lattice[c][Q:, LANES:]
                cross_sum += own_gain * lattice[c][:Q, LANES:] + cross_gain * lattice[c][Q:, :LANES]
            projected = jnp.concatenate(
                [jnp.where(own_keep, own_sum, 0.0), jnp.where(cross_keep, cross_sum, 0.0)], axis=1
            ).astype(jnp.bfloat16)
            returned = dot(squares_ref[2], projected)
            out_ref[d, pl.ds(s, Q, stride=SUB), :] = returned[:, :LANES]
            out_ref[d, pl.ds(s + PAIR, Q, stride=SUB), :] = returned[:, LANES:]
    for d in range(NCH):
        back_ref[:, d] = out_ref[d].reshape(Q, SUB, LANES).astype(jnp.bfloat16)


def flow_kernel(received_ref, sum_ref, partner_ref, flowed_hbm, flowed_buf, sems):
    upper_of, lower_of = partner_blocks(partner_ref)
    copies = []
    for c in range(NCH):
        halves = [
            jnp.concatenate([received_ref[:, half, j, c].astype(jnp.float32) for j in range(TILE_COLS)], axis=2)
            for half in range(2)
        ]
        own, crossed = interleave(*halves)
        rows = dot(lower_of, crossed.reshape(HALF, NB).astype(jnp.bfloat16))
        lower = swap_columns(rows, upper_of, lower_of)
        flowed_buf[c, :HALF] = (sum_ref[c, :HALF] + own.reshape(HALF, NB)).astype(jnp.bfloat16)
        flowed_buf[c, HALF:] = (sum_ref[c, HALF:] + lower).astype(jnp.bfloat16)
        copies.append(pltpu.make_async_copy(flowed_buf.at[c], flowed_hbm.at[c, 0], sems.at[c]))
        copies[c].start()
    for copy in copies:
        copy.wait()


def per_device(vertex, loop_matrix, own_mix, cross_mix, shells, partner, grid_index):
    f32, bf16, i32 = jnp.float32, jnp.bfloat16, jnp.int32
    shape = jax.ShapeDtypeStruct
    fetched = [
        pltpu.VMEM((NCH, NB, NB), bf16),
        pltpu.VMEM((NCH, NB, NB), bf16),
        pltpu.SemaphoreType.DMA((2, NCH)),
    ]
    partner_row = partner.reshape(1, NB)
    place = lax.axis_index(AXES).astype(i32).reshape(1)
    sent = pl.pallas_call(
        product_kernel,
        in_specs=[HBM, HBM, VMEM],
        out_specs=HBM,
        out_shape=shape(TILES, bf16),
        scratch_shapes=[*fetched, pltpu.VMEM(TILES, bf16), pltpu.SemaphoreType.DMA((NCH,))],
        compiler_params=FULL,
        name="product",
    )(vertex, loop_matrix, partner_row)
    arrived = lax.all_to_all(sent.reshape(Q, NCH, SUB, LANES), AXES, 0, 0, tiled=True)
    vertex_sum, squares, rows = pl.pallas_call(
        side_kernel,
        in_specs=[SMEM] * 5 + [HBM, HBM] + [VMEM] * 3,
        out_specs=[VMEM] * 3,
        out_shape=[shape((NCH, NB, NB), f32), shape((3, Q, Q), bf16), shape((ROWS, LANES), f32)],
        scratch_shapes=fetched,
        compiler_params=PARAMS,
        name="side",
    )(
        place, own_mix, cross_mix, shells, partner, vertex, loop_matrix, grid_index.reshape(1, Q),
        shells.reshape(TILE_COLS, LANES), partner.reshape(TILE_COLS, LANES),
    )
    back = pl.pallas_call(
        lattice_kernel,
        in_specs=[VMEM] * 3,
        out_specs=VMEM,
        out_shape=shape((Q, NCH, SUB, LANES), bf16),
        scratch_shapes=[pltpu.VMEM((NCH, Q * SUB, LANES), f32), pltpu.VMEM((NCH, Q * SUB, LANES), f32)],
        compiler_params=PARAMS,
        name="lattice",
    )(arrived, squares, rows)
    received = lax.all_to_all(back, AXES, 0, 0, tiled=True).reshape(TILES)
    return pl.pallas_call(
        flow_kernel,
        in_specs=[VMEM, VMEM, VMEM],
        out_specs=HBM,
        out_shape=shape((NCH, 1, NB, NB), bf16),
        scratch_shapes=[pltpu.VMEM((NCH, NB, NB), bf16), pltpu.SemaphoreType.DMA((NCH,))],
        compiler_params=PARAMS,
        name="flow",
    )(received, vertex_sum, partner_row)


def solution(mesh):
    split = P(None, ("mom", "bond"), None, None)
    return jax.shard_map(
        per_device, mesh=mesh, in_specs=(split, split, P(), P(), P(), P(), P()), out_specs=split, check_vma=False
    )
```

```python
import math

import jax
import jax.numpy as jnp
from jax import lax
from jax.experimental import pallas as pl
from jax.experimental.pallas import tpu as pltpu
from jax.sharding import PartitionSpec as P

G = 16
NB = 512
Q = 256
NCH = 3
HALF = NB // 2
SUB = 8
LANES = 128
TILE_COLS = NB // LANES
PAIR = SUB // 2
TILES = (HALF // SUB, 2, TILE_COLS, NCH, SUB, LANES)
AXES = ("mom", "bond")
LIMITS = 0
GAINS = LIMITS + SUB
ROWS = GAINS + SUB

CAS = [math.cos(2 * math.pi * n / G) + math.sin(2 * math.pi * n / G) for n in range(8)]
CAS[6] = 0.0

SMEM = pl.BlockSpec(memory_space=pltpu.SMEM)
VMEM = pl.BlockSpec(memory_space=pltpu.VMEM)
HBM = pl.BlockSpec(memory_space=pltpu.HBM)
FULL = pltpu.CompilerParams(vmem_limit_bytes=63 << 20)
PARAMS = pltpu.CompilerParams(vmem_limit_bytes=40 << 20)


def iota(shape, dim):
    return lax.broadcasted_iota(jnp.int32, shape, dim)


def to_bf16(flags):
    return flags.astype(jnp.float32).astype(jnp.bfloat16)


def dot(a, b):
    return jnp.dot(a, b, preferred_element_type=jnp.float32)


def partner_blocks(partner_ref):
    rows = iota((HALF, HALF), 0)
    upper_of = to_bf16(partner_ref[:, HALF:] == rows)
    lower_of = to_bf16(partner_ref[:, :HALF] == rows + HALF)
    return upper_of, lower_of


def swap_columns(x, upper_of, lower_of):
    x = x.astype(jnp.bfloat16)
    return jnp.concatenate([dot(x[:, HALF:], lower_of), dot(x[:, :HALF], upper_of)], axis=1)


def interleave(first, second):
    low = iota(first.shape, 1) < PAIR
    even = jnp.where(low, first, pltpu.roll(second, PAIR, 1))
    odd = jnp.where(low, pltpu.roll(first, PAIR, 1), second)
    return even, odd


def by_groups(x):
    return x.reshape(HALF // SUB, SUB, NB)


def product_of(vertex, loop):
    return dot(dot(vertex, loop).astype(jnp.bfloat16), vertex)


def fetch(pairs, sems):
    copies = [
        [pltpu.make_async_copy(source.at[c, 0], target.at[c], sems.at[i, c]) for i, (source, target) in enumerate(pairs)]
        for c in range(NCH)
    ]
    for group in copies:
        for copy in group:
            copy.start()
    return copies


def product_kernel(vertex_ref, loop_ref, partner_ref, sent_ref, upper_ref, lower_ref):
    @pl.when(pl.program_id(0) == 0)
    def _():
        upper_ref[...], lower_ref[...] = partner_blocks(partner_ref)

    upper_of, lower_of = upper_ref[...], lower_ref[...]
    product = product_of(vertex_ref[0, 0], loop_ref[0, 0])
    swapped = swap_columns(product[HALF:], upper_of, lower_of).astype(jnp.bfloat16)
    crossed = dot(upper_of, swapped)
    for half, rows in enumerate(interleave(by_groups(product[:HALF]), by_groups(crossed))):
        for j in range(TILE_COLS):
            sent_ref[:, half, j, 0] = rows[:, :, j * LANES : (j + 1) * LANES].astype(jnp.bfloat16)


def cas_values(phase):
    low = phase & 7
    value = jnp.full(phase.shape, CAS[0], jnp.float32)
    for n in range(1, 8):
        value = jnp.where(low == n, CAS[n], value)
    return jnp.where(phase & 8 != 0, -value, value)


def gain_lane(crossed, to, source):
    return (crossed * NCH + to) * NCH + source


def side_kernel(
    place_ref, own_mix_ref, cross_mix_ref, shells_s, partner_s, vertex_hbm, loop_hbm, grid_ref, shells_ref, partner_ref,
    sum_ref, squares_ref, rows_ref, vertex_buf, loop_buf, sems,
):
    copies = fetch([(vertex_hbm, vertex_buf), (loop_hbm, loop_buf)], sems)
    tile_row = place_ref[0] // TILE_COLS
    tile_col = place_ref[0] % TILE_COLS
    point = grid_ref[...]
    disp = iota((Q, Q), 0)
    phase = (disp // G) * (point // G) + (disp % G) * (point % G)
    plus = cas_values(phase & 15)
    squares_ref[0] = plus.astype(jnp.bfloat16)
    squares_ref[1] = cas_values((-phase) & 15).astype(jnp.bfloat16)
    squares_ref[2] = plus.T.astype(jnp.bfloat16)
    pick = to_bf16(iota((NB, LANES), 0) == partner_ref[pl.ds(tile_col, 1), :])
    crossed_row = jnp.zeros((SUB, LANES), jnp.float32)
    for j in range(TILE_COLS):
        part = to_bf16(jnp.broadcast_to(shells_ref[pl.ds(j, 1), :], (SUB, LANES)))
        crossed_row += dot(part, pick[j * LANES : (j + 1) * LANES])
    crossed_row = crossed_row[:1]
    own_row = shells_ref[pl.ds(tile_col, 1), :].astype(jnp.float32)
    for s in range(PAIR):
        bond = tile_row * PAIR + s
        rows_ref[LIMITS + s : LIMITS + s + 1, :] = own_row + shells_s[bond].astype(jnp.float32)
        rows_ref[LIMITS + PAIR + s : LIMITS + PAIR + s + 1, :] = (
            crossed_row + shells_s[partner_s[bond]].astype(jnp.float32)
        )
    lane = iota((SUB, LANES), 1)
    gains = jnp.zeros((SUB, LANES), jnp.float32)
    for d in range(NCH):
        for c in range(NCH):
            gains = jnp.where(lane == gain_lane(0, d, c), own_mix_ref[d, c] * (1.0 / Q), gains)
            gains = jnp.where(lane == gain_lane(1, d, c), cross_mix_ref[d, c] * (1.0 / Q), gains)
    rows_ref[GAINS:] = gains
    for c in range(NCH):
        for copy in copies[c]:
            copy.wait()
        vertex = vertex_buf[c]
        sum_ref[c] = vertex.astype(jnp.float32) + product_of(vertex, loop_buf[c])


def lattice_kernel(arrived_ref, squares_ref, rows_ref, back_ref, in_ref, out_ref):
    lattice_point = iota((Q, LANES), 0)
    centre_x = (lattice_point // G + G // 2) % G - G // 2
    centre_y = (lattice_point % G + G // 2) % G - G // 2
    cycle = jnp.maximum(jnp.abs(centre_x), jnp.abs(centre_y)).astype(jnp.float32)
    tables = squares_ref[:2].reshape(2 * Q, Q)
    gains = rows_ref[GAINS : GAINS + 1, :]
    for c in range(NCH):
        in_ref[c, : Q * SUB] = arrived_ref[:, c].astype(jnp.float32).reshape(Q * SUB, LANES)
    for s in range(PAIR):
        own_keep = cycle <= rows_ref[LIMITS + s : LIMITS + s + 1, :]
        cross_keep = cycle <= rows_ref[LIMITS + PAIR + s : LIMITS + PAIR + s + 1, :]
        lattice = []
        for c in range(NCH):
            own = in_ref[c, pl.ds(s, Q, stride=SUB), :].astype(jnp.bfloat16)
            crossed = in_ref[c, pl.ds(s + PAIR, Q, stride=SUB), :].astype(jnp.bfloat16)
            lattice.append(dot(tables, jnp.concatenate([own, crossed], axis=1)))
        for d in range(NCH):
            own_sum = jnp.zeros((Q, LANES), jnp.float32)
            cross_sum = jnp.zeros((Q, LANES), jnp.float32)
            for c in range(NCH):
                at = gain_lane(0, d, c)
                own_gain = gains[:, at : at + 1]
                at = gain_lane(1, d, c)
                cross_gain = gains[:, at : at + 1]
                own_sum += own_gain * lattice[c][:Q, :LANES] + cross_gain * lattice[c][Q:, LANES:]
                cross_sum += own_gain * lattice[c][:Q, LANES:] + cross_gain * lattice[c][Q:, :LANES]
            projected = jnp.concatenate(
                [jnp.where(own_keep, own_sum, 0.0), jnp.where(cross_keep, cross_sum, 0.0)], axis=1
            ).astype(jnp.bfloat16)
            returned = dot(squares_ref[2], projected)
            out_ref[d, pl.ds(s, Q, stride=SUB), :] = returned[:, :LANES]
            out_ref[d, pl.ds(s + PAIR, Q, stride=SUB), :] = returned[:, LANES:]
    for d in range(NCH):
        back_ref[:, d] = out_ref[d, : Q * SUB].reshape(Q, SUB, LANES).astype(jnp.bfloat16)


def flow_kernel(received_ref, sum_ref, partner_ref, flowed_hbm, flowed_buf, sems):
    upper_of, lower_of = partner_blocks(partner_ref)
    copies = []
    for c in range(NCH):
        halves = [
            jnp.concatenate([received_ref[:, half, j, c].astype(jnp.float32) for j in range(TILE_COLS)], axis=2)
            for half in range(2)
        ]
        own, crossed = interleave(*halves)
        rows = dot(lower_of, crossed.reshape(HALF, NB).astype(jnp.bfloat16))
        lower = swap_columns(rows, upper_of, lower_of)
        flowed_buf[c, :HALF] = (sum_ref[c, :HALF] + own.reshape(HALF, NB)).astype(jnp.bfloat16)
        flowed_buf[c, HALF:] = (sum_ref[c, HALF:] + lower).astype(jnp.bfloat16)
        copies.append(pltpu.make_async_copy(flowed_buf.at[c], flowed_hbm.at[c, 0], sems.at[c]))
        copies[c].start()
    for copy in copies:
        copy.wait()


def per_device(vertex, loop_matrix, own_mix, cross_mix, shells, partner, grid_index):
    f32, bf16, i32 = jnp.float32, jnp.bfloat16, jnp.int32
    shape = jax.ShapeDtypeStruct
    fetched = [
        pltpu.VMEM((NCH, NB, NB), bf16),
        pltpu.VMEM((NCH, NB, NB), bf16),
        pltpu.SemaphoreType.DMA((2, NCH)),
    ]
    strided = pltpu.VMEM((NCH, Q * SUB + SUB, LANES), f32)
    partner_row = partner.reshape(1, NB)
    place = lax.axis_index(AXES).astype(i32).reshape(1)
    matrix_spec = pl.BlockSpec((1, 1, NB, NB), lambda c: (c, 0, 0, 0))
    sent = pl.pallas_call(
        product_kernel,
        grid=(NCH,),
        in_specs=[matrix_spec, matrix_spec, pl.BlockSpec((1, NB), lambda c: (0, 0))],
        out_specs=pl.BlockSpec((*TILES[:3], 1, SUB, LANES), lambda c: (0, 0, 0, c, 0, 0)),
        out_shape=shape(TILES, bf16),
        scratch_shapes=[pltpu.VMEM((HALF, HALF), bf16), pltpu.VMEM((HALF, HALF), bf16)],
        compiler_params=FULL,
        name="product",
    )(vertex, loop_matrix, partner_row)
    arrived = lax.all_to_all(sent.reshape(Q, NCH, SUB, LANES), AXES, 0, 0, tiled=True)
    vertex_sum, squares, rows = pl.pallas_call(
        side_kernel,
        in_specs=[SMEM] * 5 + [HBM, HBM] + [VMEM] * 3,
        out_specs=[VMEM] * 3,
        out_shape=[shape((NCH, NB, NB), f32), shape((3, Q, Q), bf16), shape((ROWS, LANES), f32)],
        scratch_shapes=fetched,
        compiler_params=PARAMS,
        name="side",
    )(
        place, own_mix, cross_mix, shells, partner, vertex, loop_matrix, grid_index.reshape(1, Q),
        shells.reshape(TILE_COLS, LANES), partner.reshape(TILE_COLS, LANES),
    )
    back = pl.pallas_call(
        lattice_kernel,
        in_specs=[VMEM] * 3,
        out_specs=VMEM,
        out_shape=shape((Q, NCH, SUB, LANES), bf16),
        scratch_shapes=[strided, strided],
        compiler_params=PARAMS,
        name="lattice",
    )(arrived, squares, rows)
    received = lax.all_to_all(back, AXES, 0, 0, tiled=True).reshape(TILES)
    return pl.pallas_call(
        flow_kernel,
        in_specs=[VMEM, VMEM, VMEM],
        out_specs=HBM,
        out_shape=shape((NCH, 1, NB, NB), bf16),
        scratch_shapes=[pltpu.VMEM((NCH, NB, NB), bf16), pltpu.SemaphoreType.DMA((NCH,))],
        compiler_params=PARAMS,
        name="flow",
    )(received, vertex_sum, partner_row)


def solution(mesh):
    split = P(None, ("mom", "bond"), None, None)
    return jax.shard_map(
        per_device, mesh=mesh, in_specs=(split, split, P(), P(), P(), P(), P()), out_specs=split, check_vma=False
    )
```

```python
import math

import jax
import jax.numpy as jnp
from jax import lax
from jax.experimental import pallas as pl
from jax.experimental.pallas import tpu as pltpu
from jax.sharding import PartitionSpec as P

G = 16
NB = 512
Q = 256
NCH = 3
HALF = NB // 2
SUB = 8
LANES = 128
TILE_COLS = NB // LANES
PAIR = SUB // 2
TILES = (HALF // SUB, 2, TILE_COLS, NCH, SUB, LANES)
AXES = ("mom", "bond")
LIMITS = 0
GAINS = LIMITS + SUB
ROWS = GAINS + SUB

CAS = [math.cos(2 * math.pi * n / G) + math.sin(2 * math.pi * n / G) for n in range(8)]
CAS[6] = 0.0

SMEM = pl.BlockSpec(memory_space=pltpu.SMEM)
VMEM = pl.BlockSpec(memory_space=pltpu.VMEM)
HBM = pl.BlockSpec(memory_space=pltpu.HBM)
FULL = pltpu.CompilerParams(vmem_limit_bytes=63 << 20)
PARAMS = pltpu.CompilerParams(vmem_limit_bytes=40 << 20)


def iota(shape, dim):
    return lax.broadcasted_iota(jnp.int32, shape, dim)


def to_bf16(flags):
    return flags.astype(jnp.float32).astype(jnp.bfloat16)


def dot(a, b):
    return jnp.dot(a, b, preferred_element_type=jnp.float32)


def partner_blocks(partner_ref):
    rows = iota((HALF, HALF), 0)
    upper_of = to_bf16(partner_ref[:, HALF:] == rows)
    lower_of = to_bf16(partner_ref[:, :HALF] == rows + HALF)
    return upper_of, lower_of


def swap_columns(x, upper_of, lower_of):
    x = x.astype(jnp.bfloat16)
    return jnp.concatenate([dot(x[:, HALF:], lower_of), dot(x[:, :HALF], upper_of)], axis=1)


def interleave(first, second):
    low = iota(first.shape, 1) < PAIR
    even = jnp.where(low, first, pltpu.roll(second, PAIR, 1))
    odd = jnp.where(low, pltpu.roll(first, PAIR, 1), second)
    return even, odd


def by_groups(x):
    return x.reshape(HALF // SUB, SUB, NB)


def product_of(vertex, loop):
    return dot(dot(vertex, loop).astype(jnp.bfloat16), vertex)


def fetch(pairs, sems):
    copies = [
        [pltpu.make_async_copy(source.at[c, 0], target.at[c], sems.at[i, c]) for i, (source, target) in enumerate(pairs)]
        for c in range(NCH)
    ]
    for group in copies:
        for copy in group:
            copy.start()
    return copies


def product_kernel(vertex_ref, loop_ref, partner_ref, sent_ref, upper_ref, lower_ref):
    @pl.when(pl.program_id(0) == 0)
    def _():
        upper_ref[...], lower_ref[...] = partner_blocks(partner_ref)

    upper_of, lower_of = upper_ref[...], lower_ref[...]
    product = product_of(vertex_ref[0, 0], loop_ref[0, 0])
    swapped = swap_columns(product[HALF:], upper_of, lower_of).astype(jnp.bfloat16)
    crossed = dot(upper_of, swapped)
    for half, rows in enumerate(interleave(by_groups(product[:HALF]), by_groups(crossed))):
        for j in range(TILE_COLS):
            sent_ref[:, half, j, 0] = rows[:, :, j * LANES : (j + 1) * LANES].astype(jnp.bfloat16)


def cas_values(phase):
    low = phase & 7
    value = jnp.full(phase.shape, CAS[0], jnp.float32)
    for n in range(1, 8):
        value = jnp.where(low == n, CAS[n], value)
    return jnp.where(phase & 8 != 0, -value, value)


def gain_lane(crossed, to, source):
    return (crossed * NCH + to) * NCH + source


def side_kernel(
    place_ref, own_mix_ref, cross_mix_ref, shells_s, partner_s, vertex_hbm, loop_hbm, grid_ref, shells_ref, partner_ref,
    partner_row_ref, sum_ref, squares_ref, rows_ref, blocks_hbm, vertex_buf, loop_buf, sems, blocks_buf, blocks_sem,
):
    copies = fetch([(vertex_hbm, vertex_buf), (loop_hbm, loop_buf)], sems)
    blocks_buf[0], blocks_buf[1] = partner_blocks(partner_row_ref)
    blocks_copy = pltpu.make_async_copy(blocks_buf, blocks_hbm, blocks_sem)
    blocks_copy.start()
    tile_row = place_ref[0] // TILE_COLS
    tile_col = place_ref[0] % TILE_COLS
    point = grid_ref[...]
    disp = iota((Q, Q), 0)
    phase = (disp // G) * (point // G) + (disp % G) * (point % G)
    plus = cas_values(phase & 15)
    squares_ref[0] = plus.astype(jnp.bfloat16)
    squares_ref[1] = cas_values((-phase) & 15).astype(jnp.bfloat16)
    squares_ref[2] = plus.T.astype(jnp.bfloat16)
    pick = to_bf16(iota((NB, LANES), 0) == partner_ref[pl.ds(tile_col, 1), :])
    crossed_row = jnp.zeros((SUB, LANES), jnp.float32)
    for j in range(TILE_COLS):
        part = to_bf16(jnp.broadcast_to(shells_ref[pl.ds(j, 1), :], (SUB, LANES)))
        crossed_row += dot(part, pick[j * LANES : (j + 1) * LANES])
    crossed_row = crossed_row[:1]
    own_row = shells_ref[pl.ds(tile_col, 1), :].astype(jnp.float32)
    for s in range(PAIR):
        bond = tile_row * PAIR + s
        rows_ref[LIMITS + s : LIMITS + s + 1, :] = own_row + shells_s[bond].astype(jnp.float32)
        rows_ref[LIMITS + PAIR + s : LIMITS + PAIR + s + 1, :] = (
            crossed_row + shells_s[partner_s[bond]].astype(jnp.float32)
        )
    lane = iota((SUB, LANES), 1)
    gains = jnp.zeros((SUB, LANES), jnp.float32)
    for d in range(NCH):
        for c in range(NCH):
            gains = jnp.where(lane == gain_lane(0, d, c), own_mix_ref[d, c] * (1.0 / Q), gains)
            gains = jnp.where(lane == gain_lane(1, d, c), cross_mix_ref[d, c] * (1.0 / Q), gains)
    rows_ref[GAINS:] = gains
    for c in range(NCH):
        for copy in copies[c]:
            copy.wait()
        vertex = vertex_buf[c]
        sum_ref[c] = vertex.astype(jnp.float32) + product_of(vertex, loop_buf[c])
    blocks_copy.wait()


def lattice_kernel(arrived_ref, squares_ref, rows_ref, back_ref, in_ref, out_ref):
    lattice_point = iota((Q, LANES), 0)
    centre_x = (lattice_point // G + G // 2) % G - G // 2
    centre_y = (lattice_point % G + G // 2) % G - G // 2
    cycle = jnp.maximum(jnp.abs(centre_x), jnp.abs(centre_y)).astype(jnp.float32)
    tables = squares_ref[:2].reshape(2 * Q, Q)
    gains = rows_ref[GAINS : GAINS + 1, :]
    for c in range(NCH):
        in_ref[c, : Q * SUB] = arrived_ref[:, c].astype(jnp.float32).reshape(Q * SUB, LANES)
    for s in range(PAIR):
        own_keep = cycle <= rows_ref[LIMITS + s : LIMITS + s + 1, :]
        cross_keep = cycle <= rows_ref[LIMITS + PAIR + s : LIMITS + PAIR + s + 1, :]
        lattice = []
        for c in range(NCH):
            own = in_ref[c, pl.ds(s, Q, stride=SUB), :].astype(jnp.bfloat16)
            crossed = in_ref[c, pl.ds(s + PAIR, Q, stride=SUB), :].astype(jnp.bfloat16)
            lattice.append(dot(tables, jnp.concatenate([own, crossed], axis=1)))
        for d in range(NCH):
            own_sum = jnp.zeros((Q, LANES), jnp.float32)
            cross_sum = jnp.zeros((Q, LANES), jnp.float32)
            for c in range(NCH):
                at = gain_lane(0, d, c)
                own_gain = gains[:, at : at + 1]
                at = gain_lane(1, d, c)
                cross_gain = gains[:, at : at + 1]
                own_sum += own_gain * lattice[c][:Q, :LANES] + cross_gain * lattice[c][Q:, LANES:]
                cross_sum += own_gain * lattice[c][:Q, LANES:] + cross_gain * lattice[c][Q:, :LANES]
            projected = jnp.concatenate(
                [jnp.where(own_keep, own_sum, 0.0), jnp.where(cross_keep, cross_sum, 0.0)], axis=1
            ).astype(jnp.bfloat16)
            returned = dot(squares_ref[2], projected)
            out_ref[d, pl.ds(s, Q, stride=SUB), :] = returned[:, :LANES]
            out_ref[d, pl.ds(s + PAIR, Q, stride=SUB), :] = returned[:, LANES:]
    for d in range(NCH):
        back_ref[:, d] = out_ref[d, : Q * SUB].reshape(Q, SUB, LANES).astype(jnp.bfloat16)


def flow_kernel(received_ref, sum_ref, blocks_ref, flowed_hbm, flowed_buf, sems):
    upper_of, lower_of = blocks_ref[0], blocks_ref[1]
    copies = []
    for c in range(NCH):
        halves = [
            jnp.concatenate([received_ref[:, half, j, c].astype(jnp.float32) for j in range(TILE_COLS)], axis=2)
            for half in range(2)
        ]
        own, crossed = interleave(*halves)
        rows = dot(lower_of, crossed.reshape(HALF, NB).astype(jnp.bfloat16))
        lower = swap_columns(rows, upper_of, lower_of)
        flowed_buf[c, :HALF] = (sum_ref[c, :HALF] + own.reshape(HALF, NB)).astype(jnp.bfloat16)
        flowed_buf[c, HALF:] = (sum_ref[c, HALF:] + lower).astype(jnp.bfloat16)
        copies.append(pltpu.make_async_copy(flowed_buf.at[c], flowed_hbm.at[c, 0], sems.at[c]))
        copies[c].start()
    for copy in copies:
        copy.wait()


def per_device(vertex, loop_matrix, own_mix, cross_mix, shells, partner, grid_index):
    f32, bf16, i32 = jnp.float32, jnp.bfloat16, jnp.int32
    shape = jax.ShapeDtypeStruct
    fetched = [
        pltpu.VMEM((NCH, NB, NB), bf16),
        pltpu.VMEM((NCH, NB, NB), bf16),
        pltpu.SemaphoreType.DMA((2, NCH)),
    ]
    strided = pltpu.VMEM((NCH, Q * SUB + SUB, LANES), f32)
    partner_row = partner.reshape(1, NB)
    place = lax.axis_index(AXES).astype(i32).reshape(1)
    matrix_spec = pl.BlockSpec((1, 1, NB, NB), lambda c: (c, 0, 0, 0))
    sent = pl.pallas_call(
        product_kernel,
        grid=(NCH,),
        in_specs=[matrix_spec, matrix_spec, pl.BlockSpec((1, NB), lambda c: (0, 0))],
        out_specs=pl.BlockSpec((*TILES[:3], 1, SUB, LANES), lambda c: (0, 0, 0, c, 0, 0)),
        out_shape=shape(TILES, bf16),
        scratch_shapes=[pltpu.VMEM((HALF, HALF), bf16), pltpu.VMEM((HALF, HALF), bf16)],
        compiler_params=FULL,
        name="product",
    )(vertex, loop_matrix, partner_row)
    arrived = lax.all_to_all(sent.reshape(Q, NCH, SUB, LANES), AXES, 0, 0, tiled=True)
    vertex_sum, squares, rows, blocks = pl.pallas_call(
        side_kernel,
        in_specs=[SMEM] * 5 + [HBM, HBM] + [VMEM] * 4,
        out_specs=[VMEM, VMEM, VMEM, HBM],
        out_shape=[shape((NCH, NB, NB), f32), shape((3, Q, Q), bf16), shape((ROWS, LANES), f32), shape((2, HALF, HALF), bf16)],
        scratch_shapes=[*fetched, pltpu.VMEM((2, HALF, HALF), bf16), pltpu.SemaphoreType.DMA],
        compiler_params=PARAMS,
        name="side",
    )(
        place, own_mix, cross_mix, shells, partner, vertex, loop_matrix, grid_index.reshape(1, Q),
        shells.reshape(TILE_COLS, LANES), partner.reshape(TILE_COLS, LANES), partner_row,
    )
    back = pl.pallas_call(
        lattice_kernel,
        in_specs=[VMEM] * 3,
        out_specs=VMEM,
        out_shape=shape((Q, NCH, SUB, LANES), bf16),
        scratch_shapes=[strided, strided],
        compiler_params=PARAMS,
        name="lattice",
    )(arrived, squares, rows)
    received = lax.all_to_all(back, AXES, 0, 0, tiled=True).reshape(TILES)
    return pl.pallas_call(
        flow_kernel,
        in_specs=[VMEM, VMEM, VMEM],
        out_specs=HBM,
        out_shape=shape((NCH, 1, NB, NB), bf16),
        scratch_shapes=[pltpu.VMEM((NCH, NB, NB), bf16), pltpu.SemaphoreType.DMA((NCH,))],
        compiler_params=PARAMS,
        name="flow",
    )(received, vertex_sum, blocks)


def solution(mesh):
    split = P(None, ("mom", "bond"), None, None)
    return jax.shard_map(
        per_device, mesh=mesh, in_specs=(split, split, P(), P(), P(), P(), P()), out_specs=split, check_vma=False
    )
```
